32 devices in a mesh: gx: 4 (over z), gy: 4 (over y, x), gz: 2 (over core).
Axes of the slice: x: 2, y: 2, z: 4, core: 2. Of those that a mesh axis runs over, the one named last changes fastest.
Arguments:
- source_points: float32 [3, 13, 4, 16, 4, 512], P(None, None, 'gx', 'gy', 'gz'), may hold values from -3 to 3
- target_points: float32 [3, 13, 4, 16, 4, 512], P(None, None, 'gx', 'gy', 'gz'), may hold values from -3 to 3
- normals: float32 [3, 13, 4, 16, 4, 512], P(None, None, 'gx', 'gy', 'gz'), may hold values from -4 to 4
- weights: float32 [13, 4, 16, 4, 512], P(None, 'gx', 'gy', 'gz'), may hold values from 0.1 to 1
- blocks: int32 [13, 4, 16, 4], P(None, 'gx', 'gy', 'gz'), may hold values from 0 to 2
- affines: float32 [12, 4, 16, 4], P(None, 'gx', 'gy', 'gz'), may hold values from -0.5 to 0.5
- anchor: int32 [1], replicated, may hold values from 0 to 255
Outputs:
- update: float32 [12, 4, 16, 4], P(None, 'gx', 'gy', 'gz')
- residual: float32 [12, 4, 16, 4], P(None, 'gx', 'gy', 'gz')
The draws below stay inside these ranges and needn't reach their ends.
Inputs may be any that keep to these rules, and one draw needn't show every extreme that they name: `blocks`: number of 256-point correspondence blocks of the correlation; entries of correlations whose second tile lies outside the grid are not read. `anchor`: a tile index (x 16 + y) * 4 + z.
All inputs are finite; a program needn't handle non-finite values.
Results may differ from the reference program's by a relative error of at most 0.0003.
Values sent between devices are 32-bit elements; how exact they have to be, the bound alone decides.
A program may use at most 128 MiB of HBM per device.

```python
import math
import jax
import jax.numpy as jnp
from jax import lax

DIRS = 13
BLOCK = 256
MAXB = 2
ITERS = 10
PTS = 512
NX = 4
NY = 16
NZ = 4


def touch_ends(drawn, stream_key, low, largest):
    index_at = [jax.random.randint(jax.random.fold_in(stream_key, axis), (), 0, length) for axis, length in enumerate(drawn.shape)]
    widest = drawn.shape.index(max(drawn.shape))
    next_to = index_at[:widest] + [(index_at[widest] + 1) % drawn.shape[widest]] + index_at[widest + 1:]
    return drawn.at[tuple(index_at)].set(low).at[tuple(next_to)].set(largest)


def steps_of(key, shape, pieces, smallest, largest):
    loudness, own = 1.0, jax.random.fold_in(key, 6)
    for dim, parts in pieces:
        draws = jnp.exp(jax.random.uniform(jax.random.fold_in(own, dim), (parts,), jnp.float32, smallest / len(pieces), largest / len(pieces)))
        loudness = loudness * jnp.repeat(draws, shape[dim] // parts).reshape([-1 if axis == dim else 1 for axis in range(len(shape))])
    return loudness


def centred(own_key, dims, scale, most, pieces=(), kind=jnp.bfloat16):
    factor_of = steps_of(own_key, dims, pieces, -0.22, 0.18) if pieces else 1.0
    array = jax.random.normal(own_key, dims, jnp.float32) * scale * factor_of
    return jnp.minimum(jnp.maximum(array, -most), most).astype(kind)


def setup_inputs(seed: int = 0) -> dict:
    keys = jax.random.split(jax.random.key(seed), 8)
    return {
        "source_points": centred(keys[0], (3, DIRS, NX, NY, NZ, PTS), 0.5, 3.0, ((2, 4), (3, 4), (4, 2)), jnp.float32),
        "target_points": centred(keys[1], (3, DIRS, NX, NY, NZ, PTS), 0.5, 3.0, ((2, 4), (3, 4), (4, 2)), jnp.float32),
        "normals": centred(keys[2], (3, DIRS, NX, NY, NZ, PTS), 1.0, 4.0, ((2, 4), (3, 4), (4, 2)), jnp.float32),
        "weights": jnp.clip(jnp.exp(math.log(1.0) - 2.3025851 * jax.random.uniform(keys[3], (DIRS, NX, NY, NZ, PTS), jnp.float32) ** steps_of(keys[3], (DIRS, NX, NY, NZ, PTS), ((1, 4), (2, 4), (3, 2)), -0.2, 0.2)), 0.1, 1.0),
        "blocks": touch_ends(jax.random.randint(keys[4], (DIRS, NX, NY, NZ), 0, MAXB + 1), jax.random.fold_in(keys[4], 1), 0, MAXB).astype(jnp.int32),
        "affines": centred(keys[5], (12, NX, NY, NZ), 0.1, 0.5, ((1, 4), (2, 4), (3, 2)), jnp.float32),
        "anchor": jax.random.randint(keys[6], (1,), 0, NX * NY * NZ).astype(jnp.int32),
    }


SPACING = 0.5
DAMPING = 1.0
OFFSETS = ((1, 0, 0), (0, 1, 0), (0, 0, 1), (1, 1, -1), (1, -1, 1), (-1, 1, 1), (1, 1, 0), (1, 0, 1), (0, 1, 1), (1, 1, 1), (1, -1, 0), (0, 1, -1), (-1, 0, 1))


def negated(offset):
    return tuple(-part for part in offset)


def moved(values, offset, first):
    widths = [(0, 0)] * values.ndim
    for axis in range(3):
        widths[first + axis] = (1, 1)
    padded = jnp.pad(values, widths)
    picks = [slice(None)] * values.ndim
    for axis in range(3):
        length = values.shape[first + axis]
        picks[first + axis] = slice(1 + offset[axis], 1 + offset[axis] + length)
    return padded[tuple(picks)]


def lifted(points):
    return jnp.concatenate([points, jnp.ones((1,) + points.shape[1:], points.dtype)], axis=0)


def mapped(affine, lifted_points):
    matrix = affine.reshape((3, 4) + affine.shape[1:]) + jnp.eye(3, 4, dtype=affine.dtype).reshape(3, 4, 1, 1, 1)
    return jnp.einsum("cexyz,exyzp->cxyzp", matrix, lifted_points, precision=lax.Precision.HIGHEST)


def correlation_terms(source, target, normal, weight, affine_here, affine_there, offset):
    exact = lax.Precision.HIGHEST
    source_lift = lifted(source)
    target_lift = lifted(target)
    stride = jnp.asarray(offset, source.dtype).reshape(3, 1, 1, 1, 1) * SPACING
    misfit = jnp.sum(normal * (mapped(affine_here, source_lift) - mapped(affine_there, target_lift) - stride), axis=0)
    layout = (12,) + source.shape[1:]
    rows_here = (normal[:, None] * source_lift[None]).reshape(layout)
    rows_there = -(normal[:, None] * target_lift[None]).reshape(layout)
    weighted_here = rows_here * weight
    weighted_there = rows_there * weight
    block_here = jnp.einsum("axyzp,bxyzp->abxyz", weighted_here, rows_here, precision=exact)
    block_pair = jnp.einsum("axyzp,bxyzp->abxyz", weighted_here, rows_there, precision=exact)
    block_there = jnp.einsum("axyzp,bxyzp->abxyz", weighted_there, rows_there, precision=exact)
    pull_here = jnp.einsum("axyzp,xyzp->axyz", weighted_here, misfit, precision=exact)
    pull_there = jnp.einsum("axyzp,xyzp->axyz", weighted_there, misfit, precision=exact)
    return block_here, block_pair, block_there, pull_here, pull_there


def invert_blocks(blocks):
    left = blocks
    right = jnp.broadcast_to(jnp.eye(12, dtype=blocks.dtype).reshape((12, 12) + (1,) * (blocks.ndim - 2)), blocks.shape)
    for pivot in range(12):
        factor = 1.0 / left[pivot, pivot]
        row_left = left[pivot] * factor
        row_right = right[pivot] * factor
        column = left[:, pivot]
        left = left - column[:, None] * row_left[None]
        right = right - column[:, None] * row_right[None]
        left = left.at[pivot].set(row_left)
        right = right.at[pivot].set(row_right)
    return right


def reference(source_points, target_points, normals, weights, blocks, affines, anchor):
    exact = lax.Precision.HIGHEST
    grid_x = jnp.arange(NX, dtype=jnp.int32).reshape(NX, 1, 1)
    grid_y = jnp.arange(NY, dtype=jnp.int32).reshape(1, NY, 1)
    grid_z = jnp.arange(NZ, dtype=jnp.int32).reshape(1, 1, NZ)
    flat = (grid_x * NY + grid_y) * NZ + grid_z
    keep = (flat != anchor[0]).astype(jnp.float32)
    filled = jnp.ones((NX, NY, NZ), jnp.float32)
    slots = jnp.arange(PTS, dtype=jnp.int32).reshape(1, 1, 1, PTS)
    diag = jnp.zeros((12, 12, NX, NY, NZ), jnp.float32)
    pull = jnp.zeros((12, NX, NY, NZ), jnp.float32)
    pairs = []
    for index, offset in enumerate(OFFSETS):
        inside = moved(filled, offset, 0)
        live = (slots < BLOCK * blocks[index][..., None]).astype(jnp.float32) * inside[..., None]
        target = moved(target_points[:, index], offset, 1)
        affine_there = moved(affines, offset, 1)
        block_here, block_pair, block_there, pull_here, pull_there = correlation_terms(
            source_points[:, index], target, normals[:, index], weights[index] * live, affines, affine_there, offset)
        diag = diag + block_here + moved(block_there, negated(offset), 2)
        pull = pull + pull_here + moved(pull_there, negated(offset), 1)
        pairs.append(block_pair * (keep * moved(keep, offset, 0)))
    coupling = jnp.stack(pairs)
    identity = jnp.eye(12, dtype=jnp.float32).reshape(12, 12, 1, 1, 1)
    diag = keep * (diag + DAMPING * identity) + (1.0 - keep) * identity
    rhs = -(keep * pull)
    inverse = invert_blocks(diag)

    def operate(vector):
        result = jnp.einsum("abxyz,bxyz->axyz", diag, vector, precision=exact)
        for index, offset in enumerate(OFFSETS):
            result = result + jnp.einsum("abxyz,bxyz->axyz", coupling[index], moved(vector, offset, 1), precision=exact)
            sent = jnp.einsum("baxyz,bxyz->axyz", coupling[index], vector, precision=exact)
            result = result + moved(sent, negated(offset), 1)
        return result

    def precondition(vector):
        return jnp.einsum("abxyz,bxyz->axyz", inverse, vector, precision=exact)

    update = jnp.zeros_like(rhs)
    residual = rhs
    scaled = precondition(residual)
    direction = scaled
    inner = jnp.sum(residual * scaled)
    for step in range(ITERS):
        image = operate(direction)
        alpha = inner / jnp.sum(direction * image)
        update = update + alpha * direction
        residual = residual - alpha * image
        scaled = precondition(residual)
        inner_next = jnp.sum(residual * scaled)
        direction = scaled + (inner_next / inner) * direction
        inner = inner_next
    return update, residual
```

```python
import functools

import jax
import jax.numpy as jnp
import numpy as np
from jax import lax
from jax.experimental import pallas as pl
from jax.experimental.pallas import tpu as pltpu
from jax.sharding import PartitionSpec as P

BLOCK = 256
ITERS = 10
SPACING = 0.5
DAMPING = 1.0
OFFSETS = (
    (1, 0, 0),
    (0, 1, 0),
    (0, 0, 1),
    (1, 1, -1),
    (1, -1, 1),
    (-1, 1, 1),
    (1, 1, 0),
    (1, 0, 1),
    (0, 1, 1),
    (1, 1, 1),
    (1, -1, 0),
    (0, 1, -1),
    (-1, 0, 1),
)
DIRS = len(OFFSETS)
SLOTS = 16
PAIR_ROWS = 96
BACK_ROWS = 64
ROWS = PAIR_ROWS + BACK_ROWS
AXES = ("gx", "gy", "gz")
MESH = pl.DeviceIdType.MESH
VMEM_BYTES = 60 * 1024 * 1024

NORMAL_PAIRS = [(c, k) for c in range(3) for k in range(c, 3)]
POINT_PAIRS = [(e, k) for e in range(4) for k in range(e, 4)]


def normal_pair(c, k):
    return NORMAL_PAIRS.index((min(c, k), max(c, k)))


def point_pair(e, k):
    return POINT_PAIRS.index((min(e, k), max(e, k)))


def moved_targets(target):
    views = {d: target[:, d] for d in range(DIRS)}
    for axis, name in enumerate(AXES):
        dim = 1 + axis
        devices = lax.axis_size(name)
        for sign in (1, -1):
            members = [d for d in range(DIRS) if OFFSETS[d][axis] == sign]
            if not members:
                continue
            length = views[members[0]].shape[dim]
            edge = 0 if sign > 0 else length - 1
            slab = jnp.stack(
                [lax.slice_in_dim(views[d], edge, edge + 1, axis=dim) for d in members]
            )
            if sign > 0:
                links = [(i + 1, i) for i in range(devices - 1)]
            else:
                links = [(i, i + 1) for i in range(devices - 1)]
            came = lax.ppermute(slab, name, links)
            for place, d in enumerate(members):
                if sign > 0:
                    kept = lax.slice_in_dim(views[d], 1, length, axis=dim)
                    pieces = [kept, came[place]]
                else:
                    kept = lax.slice_in_dim(views[d], 0, length - 1, axis=dim)
                    pieces = [came[place], kept]
                views[d] = jnp.concatenate(pieces, axis=dim)
    return jnp.stack([views[d] for d in range(DIRS)], axis=1)


def assemble_kernel(tiles, source, target, normal, weight, lane_table, affine, out, turned, acc):
    width = source.shape[1]
    points = source.shape[2]
    for start in range(0, points, 128):
        spots = pl.ds(start, 128)
        for c in range(3):
            turned[c, spots, :] = source[c, :, spots].T
            turned[3 + c, spots, :] = target[c, :, spots].T
            turned[6 + c, spots, :] = normal[c, :, spots].T
        turned[9, spots, :] = weight[:, spots].T
    acc[...] = jnp.zeros_like(acc)
    step = 32
    limit = lane_table[3:4, :]

    def body(chunk, carry):
        base = pl.multiple_of(chunk * step, step)
        spots = pl.ds(base, step)
        p = [turned[c, spots, :] for c in range(3)] + [None]
        q = [turned[3 + c, spots, :] for c in range(3)] + [None]
        n = [turned[6 + c, spots, :] for c in range(3)]
        index = base + lax.broadcasted_iota(jnp.int32, (step, width), 0)
        w = jnp.where(index.astype(jnp.float32) < limit, turned[9, spots, :], 0.0)

        def times(left, right):
            if left is None:
                return right
            return left if right is None else left * right

        def add(row, value):
            acc[row] += jnp.sum(value.reshape(step // 8, 8, width), axis=0)

        weighted = [w * n[c] * n[k] for c, k in NORMAL_PAIRS]
        for e in range(4):
            for k in range(4):
                product = times(p[e], q[k])
                for s in range(6):
                    add(s * 16 + e * 4 + k, times(weighted[s], product))
        for first, here in ((PAIR_ROWS, q), (ROWS, p)):
            for place, (e, k) in enumerate(POINT_PAIRS):
                product = times(here[e], here[k])
                for s in range(6):
                    add(first + s * 10 + place, times(weighted[s], product))
        return carry

    lax.fori_loop(0, points // step, body, 0)

    lane = lax.broadcasted_iota(jnp.int32, (8, width), 1)
    in_pairs = lane < DIRS * tiles

    def all_slots(value):
        for span in (8, 4, 2, 1):
            value = value + pltpu.roll(value, span * tiles, 1)
        return value

    here_rows = [jnp.sum(acc[ROWS + r : ROWS + r + 8], axis=1) for r in range(0, BACK_ROWS, 8)]
    stride = []
    for c in range(3):
        for e in range(4):
            total = 0.0
            for k in range(3):
                row = normal_pair(c, k) * 10 + point_pair(e, 3)
                total = total + here_rows[row // 8][row % 8 : row % 8 + 1] * lane_table[k : k + 1, :]
            stride.append(total)
    stride += [jnp.zeros((1, width), jnp.float32)] * 4
    last_slot = lane >= (SLOTS - 1) * tiles
    for r in range(0, PAIR_ROWS, 8):
        rows = jnp.sum(acc[r : r + 8], axis=1)
        if r < 16:
            rows = rows + affine[r : r + 8, :]
            rows = jnp.where(last_slot, all_slots(jnp.concatenate(stride[r : r + 8], axis=0)), rows)
        out[r : r + 8, :] = rows
    for r in range(0, BACK_ROWS, 8):
        there = jnp.sum(acc[PAIR_ROWS + r : PAIR_ROWS + r + 8], axis=1)
        out[PAIR_ROWS + r : PAIR_ROWS + r + 8, :] = jnp.where(
            in_pairs, there, all_slots(here_rows[r // 8])
        )


def gather_kernel(sizes, mine, out, local_sem, send_sem, recv_sem, hand_sem, take_sem):
    count_x, count_y, count_z = sizes
    chips_z = count_z // 2
    chips = count_x * count_y * chips_z
    at_x, at_y, at_z = (lax.axis_index(name) for name in AXES)
    core = at_z % 2
    chip = (at_x * count_y + at_y) * chips_z + at_z // 2

    def place(which, on_core):
        z = (which % chips_z) * 2 + on_core
        rest = which // chips_z
        return rest // count_y, rest % count_y, z

    def slot(which, on_core):
        x, y, z = place(which, on_core)
        return (x * count_y + y) * count_z + z

    barrier = pltpu.get_barrier_semaphore()
    sibling = place(chip, 1 - core)

    def greet(k, carry):
        other = place((chip + k) % chips, core)
        pl.semaphore_signal(barrier, inc=1, device_id=other, device_id_type=MESH)
        return carry

    lax.fori_loop(1, chips, greet, 0)
    pl.semaphore_signal(barrier, inc=1, device_id=sibling, device_id_type=MESH)
    pl.semaphore_wait(barrier, chips)

    me = slot(chip, core)
    own = pltpu.make_async_copy(mine, out.at[me], local_sem)
    own.start()

    def outgoing(k):
        return pltpu.make_async_remote_copy(
            src_ref=mine,
            dst_ref=out.at[me],
            send_sem=send_sem.at[k],
            recv_sem=recv_sem.at[k],
            device_id=place((chip + k) % chips, core),
            device_id_type=MESH,
        )

    def handed(k):
        origin = slot((chip + chips - k) % chips, core)
        return pltpu.make_async_remote_copy(
            src_ref=out.at[origin],
            dst_ref=out.at[origin],
            send_sem=hand_sem.at[k],
            recv_sem=take_sem.at[k],
            device_id=sibling,
            device_id_type=MESH,
        )

    def first_hand():
        return pltpu.make_async_remote_copy(
            src_ref=mine,
            dst_ref=out.at[me],
            send_sem=hand_sem.at[0],
            recv_sem=take_sem.at[0],
            device_id=sibling,
            device_id_type=MESH,
        )

    def send(k, carry):
        outgoing(k).start()
        return carry

    def forward(k, carry):
        outgoing(k).wait_recv()
        handed(k).start()
        return carry

    def finish(k, carry):
        outgoing(k).wait_send()
        handed(k).wait()
        return carry

    lax.fori_loop(1, chips, send, 0)
    first_hand().start()
    lax.fori_loop(1, chips, forward, 0)
    first_hand().wait()
    lax.fori_loop(1, chips, finish, 0)
    own.wait()


def turn_kernel(tiles, gathered, out):
    width = gathered.shape[2]

    def body(chunk, carry):
        rows = pl.ds(pl.multiple_of(chunk * 8, 8), 8)
        slot = lax.broadcasted_iota(jnp.int32, (8, width), 1) // tiles
        values = [gathered[j, rows, :] for j in range(SLOTS)]
        for span in (1, 2, 4, 8):
            low = (slot & span) == 0
            fresh = list(values)
            for j in range(SLOTS):
                if j & span:
                    continue
                first, second = values[j], values[j + span]
                fresh[j] = jnp.where(low, first, pltpu.roll(second, span * tiles, 1))
                fresh[j + span] = jnp.where(
                    low, pltpu.roll(first, width - span * tiles, 1), second
                )
            values = fresh
        for j in range(SLOTS):
            out[j, rows, :] = values[j]
        return carry

    lax.fori_loop(0, ROWS // 8, body, 0)


def solve_kernel(
    bricks, devices, anchor, parts, table, update_out, residual_out, blocks, inverse, ahead, sent, image
):
    span = parts.shape[2]
    tiles = bricks[0] * bricks[1] * bricks[2]
    inner = (bricks[1] * bricks[2], bricks[2], 1)
    outer = (devices[1] * devices[2] * tiles, devices[2] * tiles, tiles)

    def pull(value, axis, sign):
        near = (sign * inner[axis]) % span
        far = (sign * (outer[axis] - (bricks[axis] - 1) * inner[axis])) % span
        row = axis * 4 + (0 if sign > 0 else 2)
        result = pltpu.roll(value, (span - far) % span, 1) * table[row + 1 : row + 2, :]
        if bricks[axis] > 1:
            result = result + pltpu.roll(value, (span - near) % span, 1) * table[row : row + 1, :]
        return result

    def all_ahead(value):
        result = []
        by_z = {0: value}
        by_yz = {}
        for dx, dy, dz in OFFSETS:
            if dz not in by_z:
                by_z[dz] = pull(value, 2, dz)
            if (dy, dz) not in by_yz:
                by_yz[dy, dz] = pull(by_z[dz], 1, dy) if dy else by_z[dz]
            result.append(pull(by_yz[dy, dz], 0, dx) if dx else by_yz[dy, dz])
        return result

    def fold(read):
        by_yz = {}
        for d, (dx, dy, dz) in enumerate(OFFSETS):
            term = read(d)
            term = pull(term, 0, -dx) if dx else term
            by_yz[dy, dz] = by_yz[dy, dz] + term if (dy, dz) in by_yz else term
        by_z = {}
        for (dy, dz), term in by_yz.items():
            term = pull(term, 1, -dy) if dy else term
            by_z[dz] = by_z[dz] + term if dz in by_z else term
        total = None
        for dz, term in by_z.items():
            term = pull(term, 2, -dz) if dz else term
            total = term if total is None else total + term
        return total

    def operate(vector, shifted):
        for d, value in enumerate(all_ahead(vector)):
            ahead[d] = value
        ahead[DIRS] = vector

        def forward(a, carry):
            total = blocks[0, a] * ahead[0]
            for d in range(1, DIRS + 1):
                total = total + blocks[d, a] * ahead[d]
            image[pl.ds(a, 1), :] = jnp.sum(total, axis=0, keepdims=True)
            return carry

        lax.fori_loop(0, 12, forward, 0)
        if shifted is None:

            def backward(d, carry):
                total = blocks[d, 0] * vector[0:1]
                for a in range(1, 12):
                    total = total + blocks[d, a] * vector[a : a + 1]
                sent[d] = total
                return carry

            lax.fori_loop(0, DIRS, backward, 0)
        else:
            for d in range(DIRS):
                total = None
                for a in range(12):
                    scale = vector[a : a + 1]
                    if a % 4 == 3 and OFFSETS[d][a // 4]:
                        scale = scale - SPACING * OFFSETS[d][a // 4]
                    term = blocks[d, a] * scale
                    total = term if total is None else total + term
                sent[d] = total
        return image[...] + fold(lambda d: sent[d])

    image[...] = jnp.zeros_like(image)
    no_rows = jnp.zeros((4, span), jnp.float32)

    def expand(d, carry):
        for c in range(3):
            for e in range(4):
                for k in range(3):
                    first = normal_pair(c, k) * 16 + e * 4
                    blocks[d, 4 * c + e, 4 * k : 4 * k + 4, :] = -parts[d, first : first + 4, :]
                blocks[d, 4 * c + e, 12:16, :] = no_rows
        return carry

    lax.fori_loop(0, DIRS, expand, 0)
    diag = parts[DIRS, PAIR_ROWS:ROWS, :] + fold(lambda d: parts[d, PAIR_ROWS:ROWS, :])
    for c in range(3):
        for e in range(4):
            for k in range(3):
                for f in range(4):
                    row = normal_pair(c, k) * 10 + point_pair(e, f)
                    blocks[DIRS, 4 * c + e, 4 * k + f : 4 * k + f + 1, :] = diag[row : row + 1]
            blocks[DIRS, 4 * c + e, 12:16, :] = no_rows

    rank = lax.broadcasted_iota(jnp.int32, (16, span), 0)
    unit = ((rank == 0) | (rank == 5) | (rank == 10)).astype(jnp.float32)
    keep = (table[12:13, :] != anchor[0].astype(jnp.float32)).astype(jnp.float32)
    matrix = parts[DIRS + 1, 0:16, :] + unit
    grad = operate(matrix, True) - SPACING * parts[DIRS + 2, 0:16, :]
    rhs = -(keep * grad)

    keep_all = jnp.broadcast_to(keep, (8, span))
    for d, value in enumerate(all_ahead(keep_all)):
        both = keep * value[0:1]

        def mask(a, carry, d=d, both=both):
            blocks[d, a] = blocks[d, a] * both
            return carry

        lax.fori_loop(0, 12, mask, 0)
    rows = []
    for a in range(12):
        eye = (rank == a).astype(jnp.float32)
        row = keep * (blocks[DIRS, a] + DAMPING * eye) + (1.0 - keep) * eye
        blocks[DIRS, a] = row
        inverse[a] = row
    for pivot in range(12):
        here = inverse[pivot]
        factor = 1.0 / here[pivot : pivot + 1]
        at_pivot = rank == pivot
        scaled_row = jnp.where(at_pivot, factor, here * factor)
        for a in range(12):
            if a == pivot:
                inverse[a] = scaled_row
            else:
                row = inverse[a]
                column = row[pivot : pivot + 1]
                inverse[a] = jnp.where(at_pivot, 0.0, row) - column * scaled_row

    def precondition(vector):
        parts_of = [jnp.sum(inverse[a] * vector, axis=0, keepdims=True) for a in range(12)]
        return jnp.concatenate(parts_of + [no_rows], axis=0)

    def dot(left, right):
        return jnp.sum(left * right, keepdims=True)

    first = precondition(rhs)

    def step(_, carry):
        update, residual, direction, inner_now = carry
        along = operate(direction, None)
        alpha = inner_now / dot(direction, along)
        update = update + alpha * direction
        residual = residual - alpha * along
        scaled = precondition(residual)
        inner_next = dot(residual, scaled)
        direction = scaled + (inner_next / inner_now) * direction
        return update, residual, direction, inner_next

    start = (jnp.zeros_like(rhs), rhs, first, dot(rhs, first))
    update, residual, _, _ = lax.fori_loop(0, ITERS, step, start)
    update_out[...] = update
    residual_out[...] = residual


def lane_masks(bricks, devices):
    shape = tuple(devices) + tuple(bricks)
    index = np.indices(shape).reshape(6, -1)
    table = np.zeros((16, index.shape[1]), np.float32)
    flat = 0
    for axis in range(3):
        outer, inner = index[axis], index[3 + axis]
        end = inner == bricks[axis] - 1
        table[4 * axis] = ~end
        table[4 * axis + 1] = end & (outer < devices[axis] - 1)
        table[4 * axis + 2] = inner > 0
        table[4 * axis + 3] = (inner == 0) & (outer > 0)
        flat = flat * (devices[axis] * bricks[axis]) + outer * bricks[axis] + inner
    table[12] = flat
    return table


def on_device(source_points, target_points, normals, weights, blocks, affines, anchor):
    bricks = source_points.shape[2:5]
    points = source_points.shape[5]
    devices = tuple(lax.axis_size(name) for name in AXES)
    count = devices[0] * devices[1] * devices[2]
    tiles = bricks[0] * bricks[1] * bricks[2]
    width = SLOTS * tiles
    span = count * tiles
    params = functools.partial(pltpu.CompilerParams, vmem_limit_bytes=VMEM_BYTES)
    vmem = pl.BlockSpec(memory_space=pltpu.VMEM)

    inside = jnp.ones((DIRS,) + bricks, jnp.float32)
    for axis, name in enumerate(AXES):
        spots = lax.axis_index(name) * bricks[axis] + np.arange(bricks[axis], dtype=np.int32)
        total = devices[axis] * bricks[axis]
        steps = np.array([offset[axis] for offset in OFFSETS], np.int32).reshape(-1, 1)
        ahead = spots.reshape(1, -1) + steps
        fits = ((ahead >= 0) & (ahead < total)).astype(jnp.float32)
        inside = inside * fits.reshape((DIRS,) + tuple(-1 if i == axis else 1 for i in range(3)))
    limit = (BLOCK * blocks.astype(jnp.float32) * inside).reshape(1, DIRS * tiles)
    strides = np.repeat(np.array(OFFSETS, np.float32).T, tiles, axis=1)
    lane_table = jnp.concatenate(
        [jnp.asarray(strides), limit, jnp.zeros((4, DIRS * tiles), jnp.float32)]
    )
    lane_table = jnp.pad(lane_table, ((0, 0), (0, width - DIRS * tiles)))
    affine = jnp.pad(
        affines.reshape(12, tiles), ((0, 4), ((DIRS + 1) * tiles, width - (DIRS + 2) * tiles))
    )

    def flat(value):
        lead = value.shape[:-5]
        value = value.reshape(lead + (DIRS * tiles, points))
        return jnp.pad(value, ((0, 0),) * len(lead) + ((0, width - DIRS * tiles), (0, 0)))

    local = pl.pallas_call(
        functools.partial(assemble_kernel, tiles),
        out_shape=jax.ShapeDtypeStruct((ROWS, width), jnp.float32),
        in_specs=[vmem] * 6,
        out_specs=vmem,
        scratch_shapes=[
            pltpu.VMEM((10, points, width), jnp.float32),
            pltpu.VMEM((ROWS + BACK_ROWS, 8, width), jnp.float32),
        ],
        compiler_params=params(),
        name="assemble",
    )(
        flat(source_points),
        flat(moved_targets(target_points)),
        flat(normals),
        flat(weights),
        lane_table,
        affine,
    )
    chips = count // 2
    gathered = pl.pallas_call(
        functools.partial(gather_kernel, devices),
        out_shape=jax.ShapeDtypeStruct((count, ROWS, width), jnp.float32),
        in_specs=[vmem],
        out_specs=vmem,
        scratch_shapes=[pltpu.SemaphoreType.DMA] + [pltpu.SemaphoreType.DMA((chips,))] * 4,
        compiler_params=params(collective_id=0, has_side_effects=True),
        name="gather",
    )(local)
    parts = pl.pallas_call(
        functools.partial(turn_kernel, tiles),
        grid=(count // SLOTS,),
        out_shape=jax.ShapeDtypeStruct((SLOTS, ROWS, span), jnp.float32),
        in_specs=[pl.BlockSpec((SLOTS, ROWS, width), lambda g: (g, 0, 0))],
        out_specs=pl.BlockSpec((SLOTS, ROWS, width), lambda g: (0, 0, g)),
        compiler_params=params(),
        name="turn",
    )(gathered)
    update, residual = pl.pallas_call(
        functools.partial(solve_kernel, bricks, devices),
        out_shape=[jax.ShapeDtypeStruct((16, span), jnp.float32)] * 2,
        in_specs=[pl.BlockSpec(memory_space=pltpu.SMEM), vmem, vmem],
        out_specs=[vmem, vmem],
        scratch_shapes=[
            pltpu.VMEM((DIRS + 1, 12, 16, span), jnp.float32),
            pltpu.VMEM((12, 16, span), jnp.float32),
            pltpu.VMEM((DIRS + 1, 16, span), jnp.float32),
            pltpu.VMEM((DIRS, 16, span), jnp.float32),
            pltpu.VMEM((16, span), jnp.float32),
        ],
        compiler_params=params(),
        name="solve",
    )(anchor, parts, jnp.asarray(lane_masks(bricks, devices)))
    me = (lax.axis_index("gx") * devices[1] + lax.axis_index("gy")) * devices[2]
    me = me + lax.axis_index("gz")

    def mine(value):
        return lax.dynamic_slice(value, (0, me * tiles), (12, tiles)).reshape((12,) + bricks)

    return mine(update), mine(residual)


def solution(mesh):
    placed = (
        P(None, None, "gx", "gy", "gz", None),
        P(None, None, "gx", "gy", "gz", None),
        P(None, None, "gx", "gy", "gz", None),
        P(None, "gx", "gy", "gz", None),
        P(None, "gx", "gy", "gz"),
        P(None, "gx", "gy", "gz"),
        P(),
    )
    return jax.shard_map(
        on_device,
        mesh=mesh,
        in_specs=placed,
        out_specs=(P(None, "gx", "gy", "gz"), P(None, "gx", "gy", "gz")),
        check_vma=False,
    )
```

```python
import functools

import jax
import jax.numpy as jnp
import numpy as np
from jax import lax
from jax.experimental import pallas as pl
from jax.experimental.pallas import tpu as pltpu
from jax.sharding import PartitionSpec as P

BLOCK = 256
ITERS = 10
SPACING = 0.5
DAMPING = 1.0
OFFSETS = (
    (1, 0, 0),
    (0, 1, 0),
    (0, 0, 1),
    (1, 1, -1),
    (1, -1, 1),
    (-1, 1, 1),
    (1, 1, 0),
    (1, 0, 1),
    (0, 1, 1),
    (1, 1, 1),
    (1, -1, 0),
    (0, 1, -1),
    (-1, 0, 1),
)
DIRS = len(OFFSETS)
SLOTS = 16
PAIR_ROWS = 96
BACK_ROWS = 64
ROWS = PAIR_ROWS + BACK_ROWS
AXES = ("gx", "gy", "gz")
MESH = pl.DeviceIdType.MESH
VMEM_BYTES = 60 * 1024 * 1024

NORMAL_PAIRS = [(c, k) for c in range(3) for k in range(c, 3)]
POINT_PAIRS = [(e, k) for e in range(4) for k in range(e, 4)]


def normal_pair(c, k):
    return NORMAL_PAIRS.index((min(c, k), max(c, k)))


def point_pair(e, k):
    return POINT_PAIRS.index((min(e, k), max(e, k)))


def grouped(count, group, body):
    def trip(i, carry):
        for j in range(group):
            body(i * group + j)
        return carry

    whole = count // group
    lax.fori_loop(0, whole, trip, 0)
    for i in range(whole * group, count):
        body(i)


def moved_targets(target):
    views = {d: target[:, d] for d in range(DIRS)}
    for axis, name in enumerate(AXES):
        dim = 1 + axis
        devices = lax.axis_size(name)
        for sign in (1, -1):
            members = [d for d in range(DIRS) if OFFSETS[d][axis] == sign]
            if not members:
                continue
            length = views[members[0]].shape[dim]
            edge = 0 if sign > 0 else length - 1
            slab = jnp.stack(
                [lax.slice_in_dim(views[d], edge, edge + 1, axis=dim) for d in members]
            )
            if sign > 0:
                links = [(i + 1, i) for i in range(devices - 1)]
            else:
                links = [(i, i + 1) for i in range(devices - 1)]
            came = lax.ppermute(slab, name, links)
            for place, d in enumerate(members):
                if sign > 0:
                    kept = lax.slice_in_dim(views[d], 1, length, axis=dim)
                    pieces = [kept, came[place]]
                else:
                    kept = lax.slice_in_dim(views[d], 0, length - 1, axis=dim)
                    pieces = [came[place], kept]
                views[d] = jnp.concatenate(pieces, axis=dim)
    return jnp.stack([views[d] for d in range(DIRS)], axis=1)


def assemble_kernel(tiles, source, target, normal, weight, lane_table, affine, out, turned, acc):
    width = source.shape[1]
    points = source.shape[2]
    for start in range(0, points, 128):
        spots = pl.ds(start, 128)
        for c in range(3):
            turned[c, spots, :] = source[c, :, spots].T
            turned[3 + c, spots, :] = target[c, :, spots].T
            turned[6 + c, spots, :] = normal[c, :, spots].T
        turned[9, spots, :] = weight[:, spots].T
    acc[...] = jnp.zeros_like(acc)
    step = 32
    limit = lane_table[3:4, :]

    def body(chunk, carry):
        base = pl.multiple_of(chunk * step, step)
        spots = pl.ds(base, step)
        p = [turned[c, spots, :] for c in range(3)] + [None]
        q = [turned[3 + c, spots, :] for c in range(3)] + [None]
        n = [turned[6 + c, spots, :] for c in range(3)]
        index = base + lax.broadcasted_iota(jnp.int32, (step, width), 0)
        w = jnp.where(index.astype(jnp.float32) < limit, turned[9, spots, :], 0.0)

        def times(left, right):
            if left is None:
                return right
            return left if right is None else left * right

        def add(row, value):
            acc[row] += jnp.sum(value.reshape(step // 8, 8, width), axis=0)

        weighted = [w * n[c] * n[k] for c, k in NORMAL_PAIRS]
        for e in range(4):
            for k in range(4):
                product = times(p[e], q[k])
                for s in range(6):
                    add(s * 16 + e * 4 + k, times(weighted[s], product))
        for first, here in ((PAIR_ROWS, q), (ROWS, p)):
            for place, (e, k) in enumerate(POINT_PAIRS):
                product = times(here[e], here[k])
                for s in range(6):
                    add(first + s * 10 + place, times(weighted[s], product))
        return carry

    lax.fori_loop(0, points // step, body, 0)

    lane = lax.broadcasted_iota(jnp.int32, (8, width), 1)
    in_pairs = lane < DIRS * tiles

    def all_slots(value):
        for span in (8, 4, 2, 1):
            value = value + pltpu.roll(value, span * tiles, 1)
        return value

    here_rows = [jnp.sum(acc[ROWS + r : ROWS + r + 8], axis=1) for r in range(0, BACK_ROWS, 8)]
    stride = []
    for c in range(3):
        for e in range(4):
            total = 0.0
            for k in range(3):
                row = normal_pair(c, k) * 10 + point_pair(e, 3)
                total = total + here_rows[row // 8][row % 8 : row % 8 + 1] * lane_table[k : k + 1, :]
            stride.append(total)
    stride += [jnp.zeros((1, width), jnp.float32)] * 4
    last_slot = lane >= (SLOTS - 1) * tiles
    for r in range(0, PAIR_ROWS, 8):
        rows = jnp.sum(acc[r : r + 8], axis=1)
        if r < 16:
            rows = rows + affine[r : r + 8, :]
            rows = jnp.where(last_slot, all_slots(jnp.concatenate(stride[r : r + 8], axis=0)), rows)
        out[r : r + 8, :] = rows
    for r in range(0, BACK_ROWS, 8):
        there = jnp.sum(acc[PAIR_ROWS + r : PAIR_ROWS + r + 8], axis=1)
        out[PAIR_ROWS + r : PAIR_ROWS + r + 8, :] = jnp.where(
            in_pairs, there, all_slots(here_rows[r // 8])
        )


def gather_kernel(sizes, mine, out, local_sem, send_sem, recv_sem, hand_sem, take_sem):
    count_x, count_y, count_z = sizes
    chips_z = count_z // 2
    chips = count_x * count_y * chips_z
    at_x, at_y, at_z = (lax.axis_index(name) for name in AXES)
    core = at_z % 2
    chip = (at_x * count_y + at_y) * chips_z + at_z // 2

    def place(which, on_core):
        z = (which % chips_z) * 2 + on_core
        rest = which // chips_z
        return rest // count_y, rest % count_y, z

    def slot(which, on_core):
        x, y, z = place(which, on_core)
        return (x * count_y + y) * count_z + z

    barrier = pltpu.get_barrier_semaphore()
    sibling = place(chip, 1 - core)

    def greet(k, carry):
        other = place((chip + k) % chips, core)
        pl.semaphore_signal(barrier, inc=1, device_id=other, device_id_type=MESH)
        return carry

    lax.fori_loop(1, chips, greet, 0)
    pl.semaphore_signal(barrier, inc=1, device_id=sibling, device_id_type=MESH)
    pl.semaphore_wait(barrier, chips)

    me = slot(chip, core)
    own = pltpu.make_async_copy(mine, out.at[me], local_sem)
    own.start()

    def outgoing(k):
        return pltpu.make_async_remote_copy(
            src_ref=mine,
            dst_ref=out.at[me],
            send_sem=send_sem.at[k],
            recv_sem=recv_sem.at[k],
            device_id=place((chip + k) % chips, core),
            device_id_type=MESH,
        )

    def handed(k):
        origin = slot((chip + chips - k) % chips, core)
        return pltpu.make_async_remote_copy(
            src_ref=out.at[origin],
            dst_ref=out.at[origin],
            send_sem=hand_sem.at[k],
            recv_sem=take_sem.at[k],
            device_id=sibling,
            device_id_type=MESH,
        )

    def first_hand():
        return pltpu.make_async_remote_copy(
            src_ref=mine,
            dst_ref=out.at[me],
            send_sem=hand_sem.at[0],
            recv_sem=take_sem.at[0],
            device_id=sibling,
            device_id_type=MESH,
        )

    def send(k, carry):
        outgoing(k).start()
        return carry

    def forward(k, carry):
        outgoing(k).wait_recv()
        handed(k).start()
        return carry

    def finish(k, carry):
        outgoing(k).wait_send()
        handed(k).wait()
        return carry

    lax.fori_loop(1, chips, send, 0)
    first_hand().start()
    lax.fori_loop(1, chips, forward, 0)
    first_hand().wait()
    lax.fori_loop(1, chips, finish, 0)
    own.wait()


def turn_kernel(tiles, gathered, out):
    width = gathered.shape[2]

    def body(chunk):
        rows = pl.ds(pl.multiple_of(chunk * 8, 8), 8)
        slot = lax.broadcasted_iota(jnp.int32, (8, width), 1) // tiles
        values = [gathered[j, rows, :] for j in range(SLOTS)]
        for span in (1, 2, 4, 8):
            low = (slot & span) == 0
            fresh = list(values)
            for j in range(SLOTS):
                if j & span:
                    continue
                first, second = values[j], values[j + span]
                fresh[j] = jnp.where(low, first, pltpu.roll(second, span * tiles, 1))
                fresh[j + span] = jnp.where(
                    low, pltpu.roll(first, width - span * tiles, 1), second
                )
            values = fresh
        for j in range(SLOTS):
            out[j, rows, :] = values[j]

    grouped(ROWS // 8, 5, body)


def solve_kernel(
    bricks, devices, anchor, parts, table, update_out, residual_out, blocks, inverse, ahead, sent, image
):
    span = parts.shape[2]
    tiles = bricks[0] * bricks[1] * bricks[2]
    group = 4 if span <= 512 else 1
    inner = (bricks[1] * bricks[2], bricks[2], 1)
    outer = (devices[1] * devices[2] * tiles, devices[2] * tiles, tiles)

    def pull(value, axis, sign):
        near = (sign * inner[axis]) % span
        far = (sign * (outer[axis] - (bricks[axis] - 1) * inner[axis])) % span
        row = axis * 4 + (0 if sign > 0 else 2)
        result = pltpu.roll(value, (span - far) % span, 1) * table[row + 1 : row + 2, :]
        if bricks[axis] > 1:
            result = result + pltpu.roll(value, (span - near) % span, 1) * table[row : row + 1, :]
        return result

    def all_ahead(value):
        result = []
        by_z = {0: value}
        by_yz = {}
        for dx, dy, dz in OFFSETS:
            if dz not in by_z:
                by_z[dz] = pull(value, 2, dz)
            if (dy, dz) not in by_yz:
                by_yz[dy, dz] = pull(by_z[dz], 1, dy) if dy else by_z[dz]
            result.append(pull(by_yz[dy, dz], 0, dx) if dx else by_yz[dy, dz])
        return result

    def fold(read):
        by_yz = {}
        for d, (dx, dy, dz) in enumerate(OFFSETS):
            term = read(d)
            term = pull(term, 0, -dx) if dx else term
            by_yz[dy, dz] = by_yz[dy, dz] + term if (dy, dz) in by_yz else term
        by_z = {}
        for (dy, dz), term in by_yz.items():
            term = pull(term, 1, -dy) if dy else term
            by_z[dz] = by_z[dz] + term if dz in by_z else term
        total = None
        for dz, term in by_z.items():
            term = pull(term, 2, -dz) if dz else term
            total = term if total is None else total + term
        return total

    def operate(vector, shifted):
        for d, value in enumerate(all_ahead(vector)):
            ahead[d] = value
        ahead[DIRS] = vector

        def forward(a):
            total = blocks[0, a] * ahead[0]
            for d in range(1, DIRS + 1):
                total = total + blocks[d, a] * ahead[d]
            image[pl.ds(a, 1), :] = jnp.sum(total, axis=0, keepdims=True)

        grouped(12, group, forward)
        if shifted is None:

            def backward(d):
                total = blocks[d, 0] * vector[0:1]
                for a in range(1, 12):
                    total = total + blocks[d, a] * vector[a : a + 1]
                sent[d] = total

            grouped(DIRS, group, backward)
        else:
            for d in range(DIRS):
                total = None
                for a in range(12):
                    scale = vector[a : a + 1]
                    if a % 4 == 3 and OFFSETS[d][a // 4]:
                        scale = scale - SPACING * OFFSETS[d][a // 4]
                    term = blocks[d, a] * scale
                    total = term if total is None else total + term
                sent[d] = total
        return image[...] + fold(lambda d: sent[d])

    image[...] = jnp.zeros_like(image)
    no_rows = jnp.zeros((4, span), jnp.float32)

    def expand(d, carry):
        for c in range(3):
            for e in range(4):
                for k in range(3):
                    first = normal_pair(c, k) * 16 + e * 4
                    blocks[d, 4 * c + e, 4 * k : 4 * k + 4, :] = -parts[d, first : first + 4, :]
                blocks[d, 4 * c + e, 12:16, :] = no_rows
        return carry

    lax.fori_loop(0, DIRS, expand, 0)
    diag = parts[DIRS, PAIR_ROWS:ROWS, :] + fold(lambda d: parts[d, PAIR_ROWS:ROWS, :])
    for c in range(3):
        for e in range(4):
            for k in range(3):
                for f in range(4):
                    row = normal_pair(c, k) * 10 + point_pair(e, f)
                    blocks[DIRS, 4 * c + e, 4 * k + f : 4 * k + f + 1, :] = diag[row : row + 1]
            blocks[DIRS, 4 * c + e, 12:16, :] = no_rows

    rank = lax.broadcasted_iota(jnp.int32, (16, span), 0)
    unit = ((rank == 0) | (rank == 5) | (rank == 10)).astype(jnp.float32)
    keep = (table[12:13, :] != anchor[0].astype(jnp.float32)).astype(jnp.float32)
    matrix = parts[DIRS + 1, 0:16, :] + unit
    grad = operate(matrix, True) - SPACING * parts[DIRS + 2, 0:16, :]
    rhs = -(keep * grad)

    keep_all = jnp.broadcast_to(keep, (8, span))
    for d, value in enumerate(all_ahead(keep_all)):
        both = keep * value[0:1]

        def mask(a, carry, d=d, both=both):
            blocks[d, a] = blocks[d, a] * both
            return carry

        lax.fori_loop(0, 12, mask, 0)
    rows = []
    for a in range(12):
        eye = (rank == a).astype(jnp.float32)
        row = keep * (blocks[DIRS, a] + DAMPING * eye) + (1.0 - keep) * eye
        blocks[DIRS, a] = row
        inverse[a] = row
    for pivot in range(12):
        here = inverse[pivot]
        factor = 1.0 / here[pivot : pivot + 1]
        at_pivot = rank == pivot
        scaled_row = jnp.where(at_pivot, factor, here * factor)
        for a in range(12):
            if a == pivot:
                inverse[a] = scaled_row
            else:
                row = inverse[a]
                column = row[pivot : pivot + 1]
                inverse[a] = jnp.where(at_pivot, 0.0, row) - column * scaled_row

    def precondition(vector):
        parts_of = [jnp.sum(inverse[a] * vector, axis=0, keepdims=True) for a in range(12)]
        return jnp.concatenate(parts_of + [no_rows], axis=0)

    def dot(left, right):
        return jnp.sum(left * right, keepdims=True)

    first = precondition(rhs)

    def step(_, carry):
        update, residual, direction, inner_now = carry
        along = operate(direction, None)
        alpha = inner_now / dot(direction, along)
        update = update + alpha * direction
        residual = residual - alpha * along
        scaled = precondition(residual)
        inner_next = dot(residual, scaled)
        direction = scaled + (inner_next / inner_now) * direction
        return update, residual, direction, inner_next

    start = (jnp.zeros_like(rhs), rhs, first, dot(rhs, first))
    update, residual, _, _ = lax.fori_loop(0, ITERS, step, start)
    update_out[...] = update
    residual_out[...] = residual


def lane_masks(bricks, devices):
    shape = tuple(devices) + tuple(bricks)
    index = np.indices(shape).reshape(6, -1)
    table = np.zeros((16, index.shape[1]), np.float32)
    flat = 0
    for axis in range(3):
        outer, inner = index[axis], index[3 + axis]
        end = inner == bricks[axis] - 1
        table[4 * axis] = ~end
        table[4 * axis + 1] = end & (outer < devices[axis] - 1)
        table[4 * axis + 2] = inner > 0
        table[4 * axis + 3] = (inner == 0) & (outer > 0)
        flat = flat * (devices[axis] * bricks[axis]) + outer * bricks[axis] + inner
    table[12] = flat
    return table


def on_device(source_points, target_points, normals, weights, blocks, affines, anchor):
    bricks = source_points.shape[2:5]
    points = source_points.shape[5]
    devices = tuple(lax.axis_size(name) for name in AXES)
    count = devices[0] * devices[1] * devices[2]
    tiles = bricks[0] * bricks[1] * bricks[2]
    width = SLOTS * tiles
    span = count * tiles
    params = functools.partial(pltpu.CompilerParams, vmem_limit_bytes=VMEM_BYTES)
    vmem = pl.BlockSpec(memory_space=pltpu.VMEM)

    inside = jnp.ones((DIRS,) + bricks, jnp.float32)
    for axis, name in enumerate(AXES):
        spots = lax.axis_index(name) * bricks[axis] + np.arange(bricks[axis], dtype=np.int32)
        total = devices[axis] * bricks[axis]
        steps = np.array([offset[axis] for offset in OFFSETS], np.int32).reshape(-1, 1)
        ahead = spots.reshape(1, -1) + steps
        fits = ((ahead >= 0) & (ahead < total)).astype(jnp.float32)
        inside = inside * fits.reshape((DIRS,) + tuple(-1 if i == axis else 1 for i in range(3)))
    limit = (BLOCK * blocks.astype(jnp.float32) * inside).reshape(1, DIRS * tiles)
    strides = np.repeat(np.array(OFFSETS, np.float32).T, tiles, axis=1)
    lane_table = jnp.concatenate(
        [jnp.asarray(strides), limit, jnp.zeros((4, DIRS * tiles), jnp.float32)]
    )
    lane_table = jnp.pad(lane_table, ((0, 0), (0, width - DIRS * tiles)))
    affine = jnp.pad(
        affines.reshape(12, tiles), ((0, 4), ((DIRS + 1) * tiles, width - (DIRS + 2) * tiles))
    )

    def flat(value):
        lead = value.shape[:-5]
        value = value.reshape(lead + (DIRS * tiles, points))
        return jnp.pad(value, ((0, 0),) * len(lead) + ((0, width - DIRS * tiles), (0, 0)))

    local = pl.pallas_call(
        functools.partial(assemble_kernel, tiles),
        out_shape=jax.ShapeDtypeStruct((ROWS, width), jnp.float32),
        in_specs=[vmem] * 6,
        out_specs=vmem,
        scratch_shapes=[
            pltpu.VMEM((10, points, width), jnp.float32),
            pltpu.VMEM((ROWS + BACK_ROWS, 8, width), jnp.float32),
        ],
        compiler_params=params(),
        name="assemble",
    )(
        flat(source_points),
        flat(moved_targets(target_points)),
        flat(normals),
        flat(weights),
        lane_table,
        affine,
    )
    chips = count // 2
    gathered = pl.pallas_call(
        functools.partial(gather_kernel, devices),
        out_shape=jax.ShapeDtypeStruct((count, ROWS, width), jnp.float32),
        in_specs=[vmem],
        out_specs=pl.BlockSpec(memory_space=pl.ANY),
        scratch_shapes=[pltpu.SemaphoreType.DMA] + [pltpu.SemaphoreType.DMA((chips,))] * 4,
        compiler_params=params(collective_id=0, has_side_effects=True),
        name="gather",
    )(local)
    parts = pl.pallas_call(
        functools.partial(turn_kernel, tiles),
        grid=(count // SLOTS,),
        out_shape=jax.ShapeDtypeStruct((SLOTS, ROWS, span), jnp.float32),
        in_specs=[pl.BlockSpec((SLOTS, ROWS, width), lambda g: (g, 0, 0))],
        out_specs=pl.BlockSpec((SLOTS, ROWS, width), lambda g: (0, 0, g)),
        compiler_params=params(),
        name="turn",
    )(gathered)
    update, residual = pl.pallas_call(
        functools.partial(solve_kernel, bricks, devices),
        out_shape=[jax.ShapeDtypeStruct((16, span), jnp.float32)] * 2,
        in_specs=[pl.BlockSpec(memory_space=pltpu.SMEM), vmem, vmem],
        out_specs=[vmem, vmem],
        scratch_shapes=[
            pltpu.VMEM((DIRS + 1, 12, 16, span), jnp.float32),
            pltpu.VMEM((12, 16, span), jnp.float32),
            pltpu.VMEM((DIRS + 1, 16, span), jnp.float32),
            pltpu.VMEM((DIRS, 16, span), jnp.float32),
            pltpu.VMEM((16, span), jnp.float32),
        ],
        compiler_params=params(),
        name="solve",
    )(anchor, parts, jnp.asarray(lane_masks(bricks, devices)))
    me = (lax.axis_index("gx") * devices[1] + lax.axis_index("gy")) * devices[2]
    me = me + lax.axis_index("gz")

    def mine(value):
        return lax.dynamic_slice(value, (0, me * tiles), (12, tiles)).reshape((12,) + bricks)

    return mine(update), mine(residual)


def solution(mesh):
    placed = (
        P(None, None, "gx", "gy", "gz", None),
        P(None, None, "gx", "gy", "gz", None),
        P(None, None, "gx", "gy", "gz", None),
        P(None, "gx", "gy", "gz", None),
        P(None, "gx", "gy", "gz"),
        P(None, "gx", "gy", "gz"),
        P(),
    )
    return jax.shard_map(
        on_device,
        mesh=mesh,
        in_specs=placed,
        out_specs=(P(None, "gx", "gy", "gz"), P(None, "gx", "gy", "gz")),
        check_vma=False,
    )
```

```python
import functools

import jax
import jax.numpy as jnp
import numpy as np
from jax import lax
from jax.experimental import pallas as pl
from jax.experimental.pallas import tpu as pltpu
from jax.sharding import PartitionSpec as P

BLOCK = 256
ITERS = 10
SPACING = 0.5
DAMPING = 1.0
OFFSETS = (
    (1, 0, 0),
    (0, 1, 0),
    (0, 0, 1),
    (1, 1, -1),
    (1, -1, 1),
    (-1, 1, 1),
    (1, 1, 0),
    (1, 0, 1),
    (0, 1, 1),
    (1, 1, 1),
    (1, -1, 0),
    (0, 1, -1),
    (-1, 0, 1),
)
DIRS = len(OFFSETS)
SLOTS = 16
PAIR_ROWS = 96
BACK_ROWS = 64
ROWS = PAIR_ROWS + BACK_ROWS
AXES = ("gx", "gy", "gz")
MESH = pl.DeviceIdType.MESH
VMEM_BYTES = 60 * 1024 * 1024

NORMAL_PAIRS = [(c, k) for c in range(3) for k in range(c, 3)]
POINT_PAIRS = [(e, k) for e in range(4) for k in range(e, 4)]


def normal_pair(c, k):
    return NORMAL_PAIRS.index((min(c, k), max(c, k)))


def point_pair(e, k):
    return POINT_PAIRS.index((min(e, k), max(e, k)))


def grouped(count, group, body):
    def trip(i, carry):
        for j in range(group):
            body(i * group + j)
        return carry

    whole = count // group
    lax.fori_loop(0, whole, trip, 0)
    for i in range(whole * group, count):
        body(i)


def moved_targets(target):
    views = {d: target[:, d] for d in range(DIRS)}
    for axis, name in enumerate(AXES):
        dim = 1 + axis
        devices = lax.axis_size(name)
        for sign in (1, -1):
            members = [d for d in range(DIRS) if OFFSETS[d][axis] == sign]
            if not members:
                continue
            length = views[members[0]].shape[dim]
            edge = 0 if sign > 0 else length - 1
            slab = jnp.stack(
                [lax.slice_in_dim(views[d], edge, edge + 1, axis=dim) for d in members]
            )
            if sign > 0:
                links = [(i + 1, i) for i in range(devices - 1)]
            else:
                links = [(i, i + 1) for i in range(devices - 1)]
            came = lax.ppermute(slab, name, links)
            for place, d in enumerate(members):
                if sign > 0:
                    kept = lax.slice_in_dim(views[d], 1, length, axis=dim)
                    pieces = [kept, came[place]]
                else:
                    kept = lax.slice_in_dim(views[d], 0, length - 1, axis=dim)
                    pieces = [came[place], kept]
                views[d] = jnp.concatenate(pieces, axis=dim)
    return jnp.stack([views[d] for d in range(DIRS)], axis=1)


def assemble_kernel(tiles, source, target, normal, weight, lane_table, affine, out, turned, acc):
    width = SLOTS * tiles
    points = source.shape[2]
    filling = jnp.zeros((width - DIRS * tiles, 128), jnp.float32)

    def turn(block):
        return jnp.concatenate([block, filling], axis=0).T

    for start in range(0, points, 128):
        spots = pl.ds(start, 128)
        for c in range(3):
            turned[c, spots, :] = turn(source[c, :, spots])
            turned[3 + c, spots, :] = turn(target[c, :, spots])
            turned[6 + c, spots, :] = turn(normal[c, :, spots])
        turned[9, spots, :] = turn(weight[:, spots])
    acc[...] = jnp.zeros_like(acc)
    step = 32
    limit = lane_table[3:4, :]

    def body(chunk, carry):
        base = pl.multiple_of(chunk * step, step)
        spots = pl.ds(base, step)
        p = [turned[c, spots, :] for c in range(3)] + [None]
        q = [turned[3 + c, spots, :] for c in range(3)] + [None]
        n = [turned[6 + c, spots, :] for c in range(3)]
        index = base + lax.broadcasted_iota(jnp.int32, (step, width), 0)
        w = jnp.where(index.astype(jnp.float32) < limit, turned[9, spots, :], 0.0)

        def times(left, right):
            if left is None:
                return right
            return left if right is None else left * right

        def add(row, value):
            acc[row] += jnp.sum(value.reshape(step // 8, 8, width), axis=0)

        weighted = [w * n[c] * n[k] for c, k in NORMAL_PAIRS]
        for e in range(4):
            for k in range(4):
                product = times(p[e], q[k])
                for s in range(6):
                    add(s * 16 + e * 4 + k, times(weighted[s], product))
        for first, here in ((PAIR_ROWS, q), (ROWS, p)):
            for place, (e, k) in enumerate(POINT_PAIRS):
                product = times(here[e], here[k])
                for s in range(6):
                    add(first + s * 10 + place, times(weighted[s], product))
        return carry

    lax.fori_loop(0, points // step, body, 0)

    lane = lax.broadcasted_iota(jnp.int32, (8, width), 1)
    in_pairs = lane < DIRS * tiles

    def all_slots(value):
        for span in (8, 4, 2, 1):
            value = value + pltpu.roll(value, span * tiles, 1)
        return value

    here_rows = [jnp.sum(acc[ROWS + r : ROWS + r + 8], axis=1) for r in range(0, BACK_ROWS, 8)]
    stride = []
    for c in range(3):
        for e in range(4):
            total = 0.0
            for k in range(3):
                row = normal_pair(c, k) * 10 + point_pair(e, 3)
                total = total + here_rows[row // 8][row % 8 : row % 8 + 1] * lane_table[k : k + 1, :]
            stride.append(total)
    stride += [jnp.zeros((1, width), jnp.float32)] * 4
    last_slot = lane >= (SLOTS - 1) * tiles
    for r in range(0, PAIR_ROWS, 8):
        rows = jnp.sum(acc[r : r + 8], axis=1)
        if r < 16:
            rows = rows + affine[r : r + 8, :]
            rows = jnp.where(last_slot, all_slots(jnp.concatenate(stride[r : r + 8], axis=0)), rows)
        out[r : r + 8, :] = rows
    for r in range(0, BACK_ROWS, 8):
        there = jnp.sum(acc[PAIR_ROWS + r : PAIR_ROWS + r + 8], axis=1)
        out[PAIR_ROWS + r : PAIR_ROWS + r + 8, :] = jnp.where(
            in_pairs, there, all_slots(here_rows[r // 8])
        )


def gather_kernel(sizes, mine, out, local_sem, send_sem, recv_sem, hand_sem, take_sem):
    count_x, count_y, count_z = sizes
    chips_z = count_z // 2
    chips = count_x * count_y * chips_z
    at_x, at_y, at_z = (lax.axis_index(name) for name in AXES)
    core = at_z % 2
    chip = (at_x * count_y + at_y) * chips_z + at_z // 2

    def place(which, on_core):
        z = (which % chips_z) * 2 + on_core
        rest = which // chips_z
        return rest // count_y, rest % count_y, z

    def slot(which, on_core):
        x, y, z = place(which, on_core)
        return (x * count_y + y) * count_z + z

    barrier = pltpu.get_barrier_semaphore()
    sibling = place(chip, 1 - core)

    def greet(k, carry):
        other = place((chip + k) % chips, core)
        pl.semaphore_signal(barrier, inc=1, device_id=other, device_id_type=MESH)
        return carry

    lax.fori_loop(1, chips, greet, 0)
    pl.semaphore_signal(barrier, inc=1, device_id=sibling, device_id_type=MESH)
    pl.semaphore_wait(barrier, chips)

    me = slot(chip, core)
    own = pltpu.make_async_copy(mine, out.at[me], local_sem)
    own.start()

    def outgoing(k):
        return pltpu.make_async_remote_copy(
            src_ref=mine,
            dst_ref=out.at[me],
            send_sem=send_sem.at[k],
            recv_sem=recv_sem.at[k],
            device_id=place((chip + k) % chips, core),
            device_id_type=MESH,
        )

    def handed(k):
        origin = slot((chip + chips - k) % chips, core)
        return pltpu.make_async_remote_copy(
            src_ref=out.at[origin],
            dst_ref=out.at[origin],
            send_sem=hand_sem.at[k],
            recv_sem=take_sem.at[k],
            device_id=sibling,
            device_id_type=MESH,
        )

    def first_hand():
        return pltpu.make_async_remote_copy(
            src_ref=mine,
            dst_ref=out.at[me],
            send_sem=hand_sem.at[0],
            recv_sem=take_sem.at[0],
            device_id=sibling,
            device_id_type=MESH,
        )

    def send(k, carry):
        outgoing(k).start()
        return carry

    def forward(k, carry):
        outgoing(k).wait_recv()
        handed(k).start()
        return carry

    def finish(k, carry):
        outgoing(k).wait_send()
        handed(k).wait()
        return carry

    first_hand().start()
    lax.fori_loop(1, chips, send, 0)
    lax.fori_loop(1, chips, forward, 0)
    first_hand().wait()
    lax.fori_loop(1, chips, finish, 0)
    own.wait()


def turn_kernel(tiles, gathered, out):
    width = gathered.shape[2]

    def body(chunk):
        rows = pl.ds(pl.multiple_of(chunk * 8, 8), 8)
        slot = lax.broadcasted_iota(jnp.int32, (8, width), 1) // tiles
        values = [gathered[j, rows, :] for j in range(SLOTS)]
        for span in (1, 2, 4, 8):
            low = (slot & span) == 0
            fresh = list(values)
            for j in range(SLOTS):
                if j & span:
                    continue
                first, second = values[j], values[j + span]
                fresh[j] = jnp.where(low, first, pltpu.roll(second, span * tiles, 1))
                fresh[j + span] = jnp.where(
                    low, pltpu.roll(first, width - span * tiles, 1), second
                )
            values = fresh
        for j in range(SLOTS):
            out[j, rows, :] = values[j]

    grouped(ROWS // 8, 5, body)


def solve_kernel(
    bricks, devices, anchor, parts, table, update_out, residual_out, blocks, inverse, ahead, sent, image
):
    span = parts.shape[2]
    tiles = bricks[0] * bricks[1] * bricks[2]
    group = DIRS if span <= 512 else 1
    inner = (bricks[1] * bricks[2], bricks[2], 1)
    outer = (devices[1] * devices[2] * tiles, devices[2] * tiles, tiles)

    def pull(value, axis, sign):
        near = (sign * inner[axis]) % span
        far = (sign * (outer[axis] - (bricks[axis] - 1) * inner[axis])) % span
        row = axis * 4 + (0 if sign > 0 else 2)
        result = pltpu.roll(value, (span - far) % span, 1) * table[row + 1 : row + 2, :]
        if bricks[axis] > 1:
            result = result + pltpu.roll(value, (span - near) % span, 1) * table[row : row + 1, :]
        return result

    def all_ahead(value):
        result = []
        by_z = {0: value}
        by_yz = {}
        for dx, dy, dz in OFFSETS:
            if dz not in by_z:
                by_z[dz] = pull(value, 2, dz)
            if (dy, dz) not in by_yz:
                by_yz[dy, dz] = pull(by_z[dz], 1, dy) if dy else by_z[dz]
            result.append(pull(by_yz[dy, dz], 0, dx) if dx else by_yz[dy, dz])
        return result

    def fold(read):
        by_yz = {}
        for d, (dx, dy, dz) in enumerate(OFFSETS):
            term = read(d)
            term = pull(term, 0, -dx) if dx else term
            by_yz[dy, dz] = by_yz[dy, dz] + term if (dy, dz) in by_yz else term
        by_z = {}
        for (dy, dz), term in by_yz.items():
            term = pull(term, 1, -dy) if dy else term
            by_z[dz] = by_z[dz] + term if dz in by_z else term
        total = None
        for dz, term in by_z.items():
            term = pull(term, 2, -dz) if dz else term
            total = term if total is None else total + term
        return total

    def operate(vector, shifted):
        for d, value in enumerate(all_ahead(vector)):
            ahead[d] = value
        ahead[DIRS] = vector

        def forward(a):
            total = blocks[0, a] * ahead[0]
            for d in range(1, DIRS + 1):
                total = total + blocks[d, a] * ahead[d]
            image[pl.ds(a, 1), :] = jnp.sum(total, axis=0, keepdims=True)

        grouped(12, min(group, 12), forward)
        if shifted is None:

            def backward(d):
                total = blocks[d, 0] * vector[0:1]
                for a in range(1, 12):
                    total = total + blocks[d, a] * vector[a : a + 1]
                sent[d] = total

            grouped(DIRS, group, backward)
        else:
            for d in range(DIRS):
                total = None
                for a in range(12):
                    scale = vector[a : a + 1]
                    if a % 4 == 3 and OFFSETS[d][a // 4]:
                        scale = scale - SPACING * OFFSETS[d][a // 4]
                    term = blocks[d, a] * scale
                    total = term if total is None else total + term
                sent[d] = total
        return image[...] + fold(lambda d: sent[d])

    image[...] = jnp.zeros_like(image)
    no_rows = jnp.zeros((4, span), jnp.float32)

    def expand(d, carry):
        for c in range(3):
            for e in range(4):
                for k in range(3):
                    first = normal_pair(c, k) * 16 + e * 4
                    blocks[d, 4 * c + e, 4 * k : 4 * k + 4, :] = -parts[d, first : first + 4, :]
                blocks[d, 4 * c + e, 12:16, :] = no_rows
        return carry

    lax.fori_loop(0, DIRS, expand, 0)
    diag = parts[DIRS, PAIR_ROWS:ROWS, :] + fold(lambda d: parts[d, PAIR_ROWS:ROWS, :])
    for c in range(3):
        for e in range(4):
            for k in range(3):
                for f in range(4):
                    row = normal_pair(c, k) * 10 + point_pair(e, f)
                    blocks[DIRS, 4 * c + e, 4 * k + f : 4 * k + f + 1, :] = diag[row : row + 1]
            blocks[DIRS, 4 * c + e, 12:16, :] = no_rows

    rank = lax.broadcasted_iota(jnp.int32, (16, span), 0)
    unit = ((rank == 0) | (rank == 5) | (rank == 10)).astype(jnp.float32)
    keep = (table[12:13, :] != anchor[0].astype(jnp.float32)).astype(jnp.float32)
    matrix = parts[DIRS + 1, 0:16, :] + unit
    grad = operate(matrix, True) - SPACING * parts[DIRS + 2, 0:16, :]
    rhs = -(keep * grad)

    keep_all = jnp.broadcast_to(keep, (8, span))
    for d, value in enumerate(all_ahead(keep_all)):
        both = keep * value[0:1]

        def mask(a, carry, d=d, both=both):
            blocks[d, a] = blocks[d, a] * both
            return carry

        lax.fori_loop(0, 12, mask, 0)
    rows = []
    for a in range(12):
        eye = (rank == a).astype(jnp.float32)
        row = keep * (blocks[DIRS, a] + DAMPING * eye) + (1.0 - keep) * eye
        blocks[DIRS, a] = row
        inverse[a] = row
    for pivot in range(12):
        here = inverse[pivot]
        factor = 1.0 / here[pivot : pivot + 1]
        at_pivot = rank == pivot
        scaled_row = jnp.where(at_pivot, factor, here * factor)
        for a in range(12):
            if a == pivot:
                inverse[a] = scaled_row
            else:
                row = inverse[a]
                column = row[pivot : pivot + 1]
                inverse[a] = jnp.where(at_pivot, 0.0, row) - column * scaled_row

    def precondition(vector):
        parts_of = [jnp.sum(inverse[a] * vector, axis=0, keepdims=True) for a in range(12)]
        return jnp.concatenate(parts_of + [no_rows], axis=0)

    def dot(left, right):
        return jnp.sum(left * right, keepdims=True)

    first = precondition(rhs)

    def step(_, carry):
        update, residual, direction, inner_now = carry
        along = operate(direction, None)
        alpha = inner_now / dot(direction, along)
        update = update + alpha * direction
        residual = residual - alpha * along
        scaled = precondition(residual)
        inner_next = dot(residual, scaled)
        direction = scaled + (inner_next / inner_now) * direction
        return update, residual, direction, inner_next

    start = (jnp.zeros_like(rhs), rhs, first, dot(rhs, first))
    update, residual, _, _ = lax.fori_loop(0, ITERS, step, start)
    update_out[...] = update
    residual_out[...] = residual


def lane_masks(bricks, devices):
    shape = tuple(devices) + tuple(bricks)
    index = np.indices(shape).reshape(6, -1)
    table = np.zeros((16, index.shape[1]), np.float32)
    flat = 0
    for axis in range(3):
        outer, inner = index[axis], index[3 + axis]
        end = inner == bricks[axis] - 1
        table[4 * axis] = ~end
        table[4 * axis + 1] = end & (outer < devices[axis] - 1)
        table[4 * axis + 2] = inner > 0
        table[4 * axis + 3] = (inner == 0) & (outer > 0)
        flat = flat * (devices[axis] * bricks[axis]) + outer * bricks[axis] + inner
    table[12] = flat
    return table


def on_device(source_points, target_points, normals, weights, blocks, affines, anchor):
    bricks = source_points.shape[2:5]
    points = source_points.shape[5]
    devices = tuple(lax.axis_size(name) for name in AXES)
    count = devices[0] * devices[1] * devices[2]
    tiles = bricks[0] * bricks[1] * bricks[2]
    width = SLOTS * tiles
    span = count * tiles
    params = functools.partial(pltpu.CompilerParams, vmem_limit_bytes=VMEM_BYTES)
    vmem = pl.BlockSpec(memory_space=pltpu.VMEM)

    inside = jnp.ones((DIRS,) + bricks, jnp.float32)
    for axis, name in enumerate(AXES):
        spots = lax.axis_index(name) * bricks[axis] + np.arange(bricks[axis], dtype=np.int32)
        total = devices[axis] * bricks[axis]
        steps = np.array([offset[axis] for offset in OFFSETS], np.int32).reshape(-1, 1)
        ahead = spots.reshape(1, -1) + steps
        fits = ((ahead >= 0) & (ahead < total)).astype(jnp.float32)
        inside = inside * fits.reshape((DIRS,) + tuple(-1 if i == axis else 1 for i in range(3)))
    limit = (BLOCK * blocks.astype(jnp.float32) * inside).reshape(1, DIRS * tiles)
    strides = np.repeat(np.array(OFFSETS, np.float32).T, tiles, axis=1)
    lane_table = jnp.concatenate(
        [jnp.asarray(strides), limit, jnp.zeros((4, DIRS * tiles), jnp.float32)]
    )
    lane_table = jnp.pad(lane_table, ((0, 0), (0, width - DIRS * tiles)))
    affine = jnp.pad(
        affines.reshape(12, tiles), ((0, 4), ((DIRS + 1) * tiles, width - (DIRS + 2) * tiles))
    )

    def flat(value):
        lead = value.shape[:-5]
        return value.reshape(lead + (DIRS * tiles, points))

    local = pl.pallas_call(
        functools.partial(assemble_kernel, tiles),
        out_shape=jax.ShapeDtypeStruct((ROWS, width), jnp.float32),
        in_specs=[vmem] * 6,
        out_specs=vmem,
        scratch_shapes=[
            pltpu.VMEM((10, points, width), jnp.float32),
            pltpu.VMEM((ROWS + BACK_ROWS, 8, width), jnp.float32),
        ],
        compiler_params=params(),
        name="assemble",
    )(
        flat(source_points),
        flat(moved_targets(target_points)),
        flat(normals),
        flat(weights),
        lane_table,
        affine,
    )
    chips = count // 2
    gathered = pl.pallas_call(
        functools.partial(gather_kernel, devices),
        out_shape=jax.ShapeDtypeStruct((count, ROWS, width), jnp.float32),
        in_specs=[vmem],
        out_specs=pl.BlockSpec(memory_space=pl.ANY),
        scratch_shapes=[pltpu.SemaphoreType.DMA] + [pltpu.SemaphoreType.DMA((chips,))] * 4,
        compiler_params=params(collective_id=0, has_side_effects=True),
        name="gather",
    )(local)
    parts = pl.pallas_call(
        functools.partial(turn_kernel, tiles),
        grid=(count // SLOTS,),
        out_shape=jax.ShapeDtypeStruct((SLOTS, ROWS, span), jnp.float32),
        in_specs=[pl.BlockSpec((SLOTS, ROWS, width), lambda g: (g, 0, 0))],
        out_specs=pl.BlockSpec((SLOTS, ROWS, width), lambda g: (0, 0, g)),
        compiler_params=params(),
        name="turn",
    )(gathered)
    update, residual = pl.pallas_call(
        functools.partial(solve_kernel, bricks, devices),
        out_shape=[jax.ShapeDtypeStruct((16, span), jnp.float32)] * 2,
        in_specs=[pl.BlockSpec(memory_space=pltpu.SMEM), vmem, vmem],
        out_specs=[vmem, vmem],
        scratch_shapes=[
            pltpu.VMEM((DIRS + 1, 12, 16, span), jnp.float32),
            pltpu.VMEM((12, 16, span), jnp.float32),
            pltpu.VMEM((DIRS + 1, 16, span), jnp.float32),
            pltpu.VMEM((DIRS, 16, span), jnp.float32),
            pltpu.VMEM((16, span), jnp.float32),
        ],
        compiler_params=params(),
        name="solve",
    )(anchor, parts, jnp.asarray(lane_masks(bricks, devices)))
    me = (lax.axis_index("gx") * devices[1] + lax.axis_index("gy")) * devices[2]
    me = me + lax.axis_index("gz")

    def mine(value):
        return lax.dynamic_slice(value, (0, me * tiles), (12, tiles)).reshape((12,) + bricks)

    return mine(update), mine(residual)


def solution(mesh):
    placed = (
        P(None, None, "gx", "gy", "gz", None),
        P(None, None, "gx", "gy", "gz", None),
        P(None, None, "gx", "gy", "gz", None),
        P(None, "gx", "gy", "gz", None),
        P(None, "gx", "gy", "gz"),
        P(None, "gx", "gy", "gz"),
        P(),
    )
    return jax.shard_map(
        on_device,
        mesh=mesh,
        in_specs=placed,
        out_specs=(P(None, "gx", "gy", "gz"), P(None, "gx", "gy", "gz")),
        check_vma=False,
    )
```
